1024 devices in a mesh: row: 16 (over y, core), col: 32 (over x, z_lo), layer: 2 (over z_hi).
Axes of the slice: x: 4, y: 8, z: 16 (z_hi: 2, z_lo: 8; z = z_hi * 8 + z_lo), core: 2. Of those that a mesh axis runs over, the one named last changes fastest.
Arguments:
- density: float32 [16, 32, 128, 9, 128], P('row', 'col'), as said below
- retained: int32 [16, 32, 2, 9, 2], P('row', 'col'), may hold values from 0 to 1, as said below
Outputs:
- purified: float32 [16, 32, 128, 9, 128], P('row', 'col', None, None, 'layer')
The draws below stay inside these ranges and needn't reach their ends.
Inputs may be any that keep to these rules, and one draw needn't show every extreme that they name: retained is 1 for the block of every atom with itself (offset index 4, equal atoms). density is zero wherever retained is 0.
All inputs are finite; a program needn't handle non-finite values.
Results may differ from the reference program's by a relative error of at most 0.00014.
Values sent between devices are 32-bit elements; how exact they have to be, the bound alone decides.
A program may use at most 32 MiB of HBM per device.

```python
import math
import jax
import jax.numpy as jnp
from jax import lax

BLOCK = 64
ATOMS = 2
NEIGH = 9
CELLS_X = 16
CELLS_Y = 32


def retained_pattern(key):
    draw_key = jax.random.fold_in(key, 101)
    levels = jax.random.randint(draw_key, (CELLS_X, CELLS_Y, ATOMS, NEIGH, ATOMS), 0, 5)
    kept_blocks = (levels < 3).astype(jnp.int32)
    center = jnp.arange(NEIGH) == NEIGH // 2
    same_atom = jnp.arange(ATOMS)[:, None] == jnp.arange(ATOMS)[None, :]
    forced = (same_atom[:, None, :] & center[None, :, None]).astype(jnp.int32)
    return jnp.maximum(kept_blocks, forced[None, None])


def draw_retained(key, part):
    return retained_pattern(key)


def draw_density(key, part):
    kept_blocks = retained_pattern(key).astype(jnp.float32)
    width_all = ATOMS * BLOCK
    spread = jnp.broadcast_to(kept_blocks[:, :, :, None, :, :, None], (CELLS_X, CELLS_Y, ATOMS, BLOCK, NEIGH, ATOMS, BLOCK))
    spread = spread.reshape(CELLS_X, CELLS_Y, width_all, NEIGH, width_all)
    noise_scale = 0.35 / math.sqrt(width_all * NEIGH * 0.6)
    noise_key = jax.random.fold_in(key, 202)
    noise_field = jax.random.normal(noise_key, (CELLS_X, CELLS_Y, width_all, NEIGH, width_all), jnp.float32)
    diag_key = jax.random.fold_in(key, 404)
    levels = jax.random.uniform(diag_key, (CELLS_X, CELLS_Y, width_all), jnp.float32, 0.0, 1.0)
    identity = (jnp.arange(width_all)[:, None] == jnp.arange(width_all)[None, :]).astype(jnp.float32)
    center = (jnp.arange(NEIGH) == NEIGH // 2).astype(jnp.float32)
    diagonal = levels[:, :, :, None, None] * center[None, None, None, :, None] * identity[None, None, :, None, :]
    return noise_field * noise_scale * spread + diagonal


def setup_inputs(seed: int = 0) -> dict:
    key_list = jax.random.split(jax.random.key(seed), 3)
    return {
        "density": draw_density(jax.random.fold_in(key_list[2], 71), 0),
        "retained": draw_retained(jax.random.fold_in(key_list[2], 71), 0),
    }


def expand_pattern(retained):
    atom_count = retained.shape[2]
    full_width = atom_count * BLOCK
    as_float = retained.astype(jnp.float32)
    spread = jnp.broadcast_to(as_float[:, :, :, None, :, :, None], (CELLS_X, CELLS_Y, atom_count, BLOCK, NEIGH, atom_count, BLOCK))
    return spread.reshape(CELLS_X, CELLS_Y, full_width, NEIGH, full_width)


def multiply(first_factor, second_factor, keeper):
    partial_sums = [None] * 9
    for step_x in (-1, 0, 1):
        for step_y in (-1, 0, 1):
            source_index = 3 * (step_x + 1) + (step_y + 1)
            shifted_factor = jnp.roll(second_factor, (-step_x, -step_y), (0, 1))
            for reach_x in (-1, 0, 1):
                for reach_y in (-1, 0, 1):
                    target_x = step_x + reach_x
                    target_y = step_y + reach_y
                    if abs(target_x) <= 1 and abs(target_y) <= 1:
                        reach_index = 3 * (reach_x + 1) + (reach_y + 1)
                        target_index = 3 * (target_x + 1) + (target_y + 1)
                        product_term = jnp.einsum("xyab,xybc->xyac", first_factor[:, :, :, source_index, :], shifted_factor[:, :, :, reach_index, :], precision=lax.Precision.HIGHEST)
                        if partial_sums[target_index] is None:
                            partial_sums[target_index] = product_term
                        else:
                            partial_sums[target_index] = partial_sums[target_index] + product_term
    return jnp.stack(partial_sums, axis=3) * keeper


def reference(density, retained):
    keeper = expand_pattern(retained)
    square = multiply(density, density, keeper)
    cube_term = multiply(square, density, keeper)
    return 3.0 * square - 2.0 * cube_term
```

```python
import jax
import jax.numpy as jnp
from jax import lax
from jax.experimental import pallas as pl
from jax.experimental.pallas import tpu as pltpu
from jax.sharding import PartitionSpec as P

MESH = pl.DeviceIdType.MESH
RUN = 8


def reach(step):
    return max(0, 1 - step), 3 - abs(step - 1)


def split(value):
    high = value.astype(jnp.bfloat16)
    low = (value - high.astype(jnp.float32)).astype(jnp.bfloat16)
    return high, low


def kernel(rows, cols, run, p_hbm, kept, out_ref, got, high, low, left, square, cube,
           local_sem, send_z, recv_z, send_row, recv_row, send_fwd, recv_fwd):
    row, col, layer = lax.axis_index("row"), lax.axis_index("col"), lax.axis_index("layer")
    parity = lax.rem(row, 2)
    far, near = 2 * parity, 2 - 2 * parity
    far_dev = (lax.rem(row + far - 1 + rows, rows), col, layer)
    near_dev = (lax.rem(row + near - 1 + rows, rows), col, layer)
    place = lax.rem(col, run)
    after = (row, lax.rem(col + 1, cols), lax.rem(layer + lax.div(place + 1, run), 2))
    before = (row, lax.rem(col + cols - 1, cols), lax.rem(layer + lax.div(run - place, run), 2))

    barrier = pltpu.get_barrier_semaphore()
    for device in (after, before, far_dev, near_dev):
        pl.semaphore_signal(barrier, inc=1, device_id=device, device_id_type=MESH)
    own = pltpu.make_async_copy(p_hbm, got.at[1, 1], local_sem)
    own.start()
    pl.semaphore_wait(barrier, 4)

    def remote(src, dst, sems, rsems, place, device):
        return pltpu.make_async_remote_copy(
            src_ref=src, dst_ref=dst, send_sem=sems.at[place], recv_sem=rsems.at[place],
            device_id=device, device_id_type=MESH)

    sides = ((before, 2, 0), (after, 0, 1))
    z_copies = {}
    for part, which in enumerate((1, far, near)):
        for side, (device, step, start) in enumerate(sides):
            z_copies[part, side] = remote(
                p_hbm.at[which, pl.ds(start, 2)], got.at[1, step, which, pl.ds(start, 2)],
                send_z, recv_z, (part, side), device)
    row_copies = [
        remote(p_hbm.at[pl.ds(parity, 2)], got.at[near, 1, pl.ds(parity, 2)],
               send_row, recv_row, 0, far_dev),
        remote(p_hbm.at[pl.ds(1 - parity, 2)], got.at[far, 1, pl.ds(1 - parity, 2)],
               send_row, recv_row, 1, near_dev),
    ]
    z_copies[0, 0].start()
    z_copies[0, 1].start()
    row_copies[0].start()
    row_copies[1].start()
    for part in (1, 2):
        for side in (0, 1):
            z_copies[part, side].start()

    def forward(slot, which, side, device, place):
        step, start = sides[side][1:]
        return remote(got.at[1, step, which, pl.ds(start, 2)],
                      got.at[place, step, which, pl.ds(start, 2)],
                      send_fwd, recv_fwd, (slot, side), device)

    def load(step_x, step_y):
        first_x, count_x = reach(step_x)
        first_y, count_y = reach(step_y)
        for rx in range(first_x, first_x + count_x):
            for ry in range(first_y, first_y + count_y):
                h, l = split(got[step_x, step_y, rx, ry])
                high[step_x, step_y, rx, :, 128 * ry : 128 * ry + 128] = h
                low[step_x, step_y, rx, :, 128 * ry : 128 * ry + 128] = l

    def multiply(total, step_x, step_y):
        first_x, count_x = reach(step_x)
        first_y, count_y = reach(step_y)
        factor = left[3 * step_x + step_y]
        lanes = pl.ds(128 * first_y, 128 * count_y)
        target = pl.ds(128 * (first_y + step_y - 1), 128 * count_y)
        for rx in range(first_x, first_x + count_x):
            both = jnp.dot(factor, high[step_x, step_y, rx, :, lanes],
                           preferred_element_type=jnp.float32)
            rest = jnp.dot(factor[:128], low[step_x, step_y, rx, :, lanes],
                           preferred_element_type=jnp.float32)
            total[rx + step_x - 1, :, target] += both[:128] + (both[128:] + rest)

    square[...] = jnp.zeros_like(square)
    cube[...] = jnp.zeros_like(cube)
    own.wait()
    load(1, 1)
    for index in range(9):
        left[index, :128] = high[1, 1, index // 3, :, 128 * (index % 3) : 128 * (index % 3) + 128]
        left[index, 128:] = low[1, 1, index // 3, :, 128 * (index % 3) : 128 * (index % 3) + 128]
    multiply(square, 1, 1)

    forwards = []

    def send_on(slot, which, side, device, place):
        copy = forward(slot, which, side, device, place)
        copy.start()
        forwards.append(copy)

    for side in (0, 1):
        z_copies[0, side].wait_recv()
        send_on(0, 1, side, far_dev, near)
        send_on(1, 1, side, near_dev, far)
    row_copies[1].wait_recv()
    row_copies[0].wait_recv()
    for step_x in (0, 2):
        load(step_x, 1)
        multiply(square, step_x, 1)
    for side in (0, 1):
        z_copies[1, side].wait_recv()
        send_on(2, far, side, far_dev, near)
    for side in (0, 1):
        z_copies[2, side].wait_recv()
        send_on(3, near, side, near_dev, far)
    for step_y in (0, 2):
        load(1, step_y)
        multiply(square, 1, step_y)
    for copy in forwards:
        copy.wait_recv()
    for step_x in (0, 2):
        for step_y in (0, 2):
            load(step_x, step_y)
            multiply(square, step_x, step_y)

    upper = lax.broadcasted_iota(jnp.int32, (128, 128), 0) < 64
    first = lax.broadcasted_iota(jnp.int32, (128, 128), 1) < 64

    def keep(index):
        scale = [[kept[a, b, index].astype(jnp.float32) for b in range(2)] for a in range(2)]
        return jnp.where(upper, jnp.where(first, scale[0][0], scale[0][1]),
                         jnp.where(first, scale[1][0], scale[1][1]))

    for index in range(9):
        lanes = pl.ds(128 * (index % 3), 128)
        value = square[index // 3, :, lanes] * keep(index)
        square[index // 3, :, lanes] = value
        h, l = split(value)
        left[index, :128] = h
        left[index, 128:] = l
    for index in range(9):
        multiply(cube, index // 3, index % 3)
    for index in range(9):
        lanes = pl.ds(128 * (index % 3), 128)
        value = 3.0 * square[index // 3, :, lanes] - 2.0 * (cube[index // 3, :, lanes] * keep(index))
        out_ref[index] = jnp.where(layer == 0, value[:, :64], value[:, 64:])

    for copy in list(z_copies.values()) + row_copies + forwards:
        copy.wait_send()


def solution(mesh):
    sizes = dict(mesh.shape)
    rows, cols = sizes["row"], sizes["col"]
    run = min(RUN, cols)

    def whole(*args):
        kernel(rows, cols, run, *args)

    def body(density, retained):
        blocks = density[0, 0].transpose(1, 0, 2).reshape(3, 3, 128, 128)
        kept = retained[0, 0].transpose(0, 2, 1)
        f32, bf16 = jnp.float32, jnp.bfloat16
        dma = pltpu.SemaphoreType.DMA
        result = pl.pallas_call(
            whole,
            out_shape=jax.ShapeDtypeStruct((9, 128, 64), f32),
            in_specs=[pl.BlockSpec(memory_space=pl.ANY), pl.BlockSpec(memory_space=pltpu.SMEM)],
            out_specs=pl.BlockSpec(memory_space=pltpu.VMEM),
            scratch_shapes=[
                pltpu.VMEM((3, 3, 3, 3, 128, 128), f32),
                pltpu.VMEM((3, 3, 3, 128, 384), bf16),
                pltpu.VMEM((3, 3, 3, 128, 384), bf16),
                pltpu.VMEM((9, 256, 128), bf16),
                pltpu.VMEM((3, 128, 384), f32),
                pltpu.VMEM((3, 128, 384), f32),
                dma, dma((3, 2)), dma((3, 2)), dma((2,)), dma((2,)), dma((4, 2)), dma((4, 2)),
            ],
            compiler_params=pltpu.CompilerParams(
                collective_id=0, has_side_effects=True, vmem_limit_bytes=40 << 20),
        )(blocks, kept)
        return result.transpose(1, 0, 2)[None, None]

    placed = P("row", "col", None, None, None)
    return jax.shard_map(body, mesh=mesh, in_specs=(placed, placed),
                         out_specs=P("row", "col", None, None, "layer"), check_vma=False)
```

```python
import jax
import jax.numpy as jnp
from jax import lax
from jax.experimental import pallas as pl
from jax.experimental.pallas import tpu as pltpu
from jax.sharding import PartitionSpec as P

MESH = pl.DeviceIdType.MESH
RUN = 8


def reach(step):
    return max(0, 1 - step), 3 - abs(step - 1)


def split(value):
    high = value.astype(jnp.bfloat16)
    low = (value - high.astype(jnp.float32)).astype(jnp.bfloat16)
    return high, low


def kernel(rows, cols, run, p_hbm, kept_hbm, out_ref, kept, got, high, low, left, left_cube, square,
           cube, local_sem, kept_sem, send_z, recv_z, send_row, recv_row, send_fwd, recv_fwd):
    row, col, layer = lax.axis_index("row"), lax.axis_index("col"), lax.axis_index("layer")
    parity = lax.rem(row, 2)
    far, near = 2 * parity, 2 - 2 * parity
    far_dev = (lax.rem(row + far - 1 + rows, rows), col, layer)
    near_dev = (lax.rem(row + near - 1 + rows, rows), col, layer)
    place = lax.rem(col, run)
    after = (row, lax.rem(col + 1, cols), lax.rem(layer + lax.div(place + 1, run), 2))
    before = (row, lax.rem(col + cols - 1, cols), lax.rem(layer + lax.div(run - place, run), 2))

    barrier = pltpu.get_barrier_semaphore()
    for device in (after, before, far_dev, near_dev):
        pl.semaphore_signal(barrier, inc=1, device_id=device, device_id_type=MESH)
    own = pltpu.make_async_copy(p_hbm, got.at[1, 1], local_sem)
    own.start()
    pattern = pltpu.make_async_copy(kept_hbm, kept, kept_sem)
    pattern.start()
    pl.semaphore_wait(barrier, 4)

    def remote(src, dst, sems, rsems, place, device):
        return pltpu.make_async_remote_copy(
            src_ref=src, dst_ref=dst, send_sem=sems.at[place], recv_sem=rsems.at[place],
            device_id=device, device_id_type=MESH)

    sides = ((before, 2, 0), (after, 0, 1))
    z_copies = {}
    for part, which in enumerate((1, far, near)):
        for side, (device, step, start) in enumerate(sides):
            z_copies[part, side] = remote(
                p_hbm.at[which, pl.ds(start, 2)], got.at[1, step, which, pl.ds(start, 2)],
                send_z, recv_z, (part, side), device)
    row_copies = [
        remote(p_hbm.at[pl.ds(parity, 2)], got.at[near, 1, pl.ds(parity, 2)],
               send_row, recv_row, 0, far_dev),
        remote(p_hbm.at[pl.ds(1 - parity, 2)], got.at[far, 1, pl.ds(1 - parity, 2)],
               send_row, recv_row, 1, near_dev),
    ]
    z_copies[0, 0].start()
    z_copies[0, 1].start()
    row_copies[0].start()
    row_copies[1].start()
    for part in (1, 2):
        for side in (0, 1):
            z_copies[part, side].start()

    def forward(slot, which, side, device, place):
        step, start = sides[side][1:]
        return remote(got.at[1, step, which, pl.ds(start, 2)],
                      got.at[place, step, which, pl.ds(start, 2)],
                      send_fwd, recv_fwd, (slot, side), device)

    def load(step_x, step_y, rx):
        first, count = reach(step_y)
        for ry in range(first, first + count):
            h, l = split(got[step_x, step_y, rx, ry])
            high[step_x, step_y, rx, :, 128 * ry : 128 * ry + 128] = h
            low[step_x, step_y, rx, :, 128 * ry : 128 * ry + 128] = l

    def multiply(total, factors, step_x, step_y, rx):
        first, count = reach(step_y)
        factor = factors[step_x, step_y]
        lanes = pl.ds(128 * first, 128 * count)
        target = pl.ds(128 * (first + step_y - 1), 128 * count)
        both = jnp.dot(factor, high[step_x, step_y, rx, :, lanes],
                       preferred_element_type=jnp.float32)
        rest = jnp.dot(factor[:128], low[step_x, step_y, rx, :, lanes],
                       preferred_element_type=jnp.float32)
        total[rx + step_x - 1, :, target] += both[:128] + (both[128:] + rest)

    def add_square(step_x, step_y, rx):
        load(step_x, step_y, rx)
        multiply(square, left, step_x, step_y, rx)

    def add_cube(step_x, step_y, rx):
        multiply(cube, left_cube, step_x, step_y, rx)

    upper = lax.broadcasted_iota(jnp.int32, (128, 128), 0) < 64
    first_half = lax.broadcasted_iota(jnp.int32, (128, 128), 1) < 64

    def keep(index):
        scale = [[kept[a, b, index].astype(jnp.float32) for b in range(2)] for a in range(2)]
        return jnp.where(upper, jnp.where(first_half, scale[0][0], scale[0][1]),
                         jnp.where(first_half, scale[1][0], scale[1][1]))

    def finish_square(target_x):
        for target_y in range(3):
            lanes = pl.ds(128 * target_y, 128)
            value = square[target_x, :, lanes] * keep(3 * target_x + target_y)
            square[target_x, :, lanes] = value
            h, l = split(value)
            left_cube[target_x, target_y, :128] = h
            left_cube[target_x, target_y, 128:] = l

    square[...] = jnp.zeros_like(square)
    cube[...] = jnp.zeros_like(cube)
    own.wait()
    pattern.wait()
    for rx in range(3):
        load(1, 1, rx)
        for ry in range(3):
            lanes = pl.ds(128 * ry, 128)
            left[rx, ry, :128] = high[1, 1, rx, :, lanes]
            left[rx, ry, 128:] = low[1, 1, rx, :, lanes]
    for rx in range(3):
        multiply(square, left, 1, 1, rx)
    row_copies[1].wait_recv()
    add_square(near, 1, 1)
    add_square(near, 1, far)

    forwards = {}

    def send_on(slot, which, side, device, place):
        copy = forward(slot, which, side, device, place)
        copy.start()
        forwards[slot, side] = copy

    for side in (0, 1):
        z_copies[0, side].wait_recv()
        send_on(0, 1, side, far_dev, near)
        send_on(1, 1, side, near_dev, far)
    for step_y in (2, 0):
        add_square(1, step_y, 1)
    row_copies[0].wait_recv()
    add_square(far, 1, 1)
    add_square(far, 1, near)
    for side in (0, 1):
        z_copies[1, side].wait_recv()
        send_on(2, far, side, far_dev, near)
    for step_y in (2, 0):
        add_square(1, step_y, far)
    for side in (0, 1):
        forwards[1, side].wait_recv()
    for step_y in (2, 0):
        add_square(near, step_y, 1)
    for side in (0, 1):
        z_copies[2, side].wait_recv()
        send_on(3, near, side, near_dev, far)
    for step_y in (2, 0):
        add_square(1, step_y, near)
    finish_square(near)
    for step_y in range(3):
        if step_y == 1:
            add_cube(near, 1, far)
        add_cube(near, step_y, 1)
    for side in (0, 1):
        forwards[0, side].wait_recv()
    for step_y in (2, 0):
        add_square(far, step_y, 1)
    finish_square(far)
    for step_y in range(3):
        if step_y == 1:
            add_cube(far, 1, near)
        add_cube(far, step_y, 1)
    for side in (0, 1):
        forwards[3, side].wait_recv()
    for step_y in (2, 0):
        add_square(near, step_y, far)
        add_cube(near, step_y, far)
    for side in (0, 1):
        forwards[2, side].wait_recv()
    for step_y in (2, 0):
        add_square(far, step_y, near)
        add_cube(far, step_y, near)
    finish_square(1)
    for step_y in range(3):
        for rx in range(3):
            add_cube(1, step_y, rx)
    for index in range(9):
        lanes = pl.ds(128 * (index % 3), 128)
        value = 3.0 * square[index // 3, :, lanes] - 2.0 * (cube[index // 3, :, lanes] * keep(index))
        out_ref[index] = jnp.where(layer == 0, value[:, :64], value[:, 64:])

    for copy in list(z_copies.values()) + row_copies + list(forwards.values()):
        copy.wait_send()


def solution(mesh):
    sizes = dict(mesh.shape)
    rows, cols = sizes["row"], sizes["col"]
    run = min(RUN, cols)

    def whole(*args):
        kernel(rows, cols, run, *args)

    def body(density, retained):
        blocks = density[0, 0].transpose(1, 0, 2).reshape(3, 3, 128, 128)
        kept = retained[0, 0].transpose(0, 2, 1)
        f32, bf16 = jnp.float32, jnp.bfloat16
        dma = pltpu.SemaphoreType.DMA
        result = pl.pallas_call(
            whole,
            out_shape=jax.ShapeDtypeStruct((9, 128, 64), f32),
            in_specs=[pl.BlockSpec(memory_space=pl.ANY), pl.BlockSpec(memory_space=pl.ANY)],
            out_specs=pl.BlockSpec(memory_space=pltpu.VMEM),
            scratch_shapes=[
                pltpu.SMEM((2, 2, 9), jnp.int32),
                pltpu.VMEM((3, 3, 3, 3, 128, 128), f32),
                pltpu.VMEM((3, 3, 3, 128, 384), bf16),
                pltpu.VMEM((3, 3, 3, 128, 384), bf16),
                pltpu.VMEM((3, 3, 256, 128), bf16),
                pltpu.VMEM((3, 3, 256, 128), bf16),
                pltpu.VMEM((3, 128, 384), f32),
                pltpu.VMEM((3, 128, 384), f32),
                dma, dma, dma((3, 2)), dma((3, 2)), dma((2,)), dma((2,)), dma((4, 2)), dma((4, 2)),
            ],
            compiler_params=pltpu.CompilerParams(
                collective_id=0, has_side_effects=True, vmem_limit_bytes=67043328),
        )(blocks, kept)
        return result.transpose(1, 0, 2)[None, None]

    placed = P("row", "col", None, None, None)
    return jax.shard_map(body, mesh=mesh, in_specs=(placed, placed),
                         out_specs=P("row", "col", None, None, "layer"), check_vma=False)
```

```python
import jax
import jax.numpy as jnp
from jax import lax
from jax.experimental import pallas as pl
from jax.experimental.pallas import tpu as pltpu
from jax.sharding import PartitionSpec as P

MESH = pl.DeviceIdType.MESH
RUN = 8


def reach(step):
    return max(0, 1 - step), 3 - abs(step - 1)


def split(value):
    high = value.astype(jnp.bfloat16)
    low = (value - high.astype(jnp.float32)).astype(jnp.bfloat16)
    return high, low


def kernel(rows, cols, run, p_hbm, kept_hbm, out_ref, kept, got, high, low, left, left_cube, square,
           cube, local_sem, kept_sem, ready, send_z, recv_z, send_row, recv_row, send_fwd, recv_fwd):
    row, col, layer = lax.axis_index("row"), lax.axis_index("col"), lax.axis_index("layer")
    parity = lax.rem(row, 2)
    far, near = 2 * parity, 2 - 2 * parity
    far_dev = (lax.rem(row + far - 1 + rows, rows), col, layer)
    near_dev = (lax.rem(row + near - 1 + rows, rows), col, layer)
    place = lax.rem(col, run)
    after = (row, lax.rem(col + 1, cols), lax.rem(layer + lax.div(place + 1, run), 2))
    before = (row, lax.rem(col + cols - 1, cols), lax.rem(layer + lax.div(run - place, run), 2))

    bottom = jnp.logical_and(layer == 0, place == 0)

    barrier = pltpu.get_barrier_semaphore()
    for device in (before, far_dev, near_dev):
        pl.semaphore_signal(barrier, inc=1, device_id=device, device_id_type=MESH)

    own = pltpu.make_async_copy(p_hbm, got.at[1, 1], local_sem)
    own.start()
    pattern = pltpu.make_async_copy(kept_hbm, kept, kept_sem)
    pattern.start()
    pl.semaphore_wait(barrier, 3)

    def remote(src, dst, sems, rsems, place, device):
        return pltpu.make_async_remote_copy(
            src_ref=src, dst_ref=dst, send_sem=sems.at[place], recv_sem=rsems.at[place],
            device_id=device, device_id_type=MESH)

    parts = ((1, 0, 2), (far, 0, 1), (far, 1, 1), (near, 0, 1), (near, 1, 1))
    sides = ((before, 2, 0), (after, 0, 1))

    def z_copy(part, side, device):
        which, offset, count = parts[part]
        step, start = sides[side][1:]
        ys = pl.ds(start + offset, count)
        return remote(p_hbm.at[which, ys], got.at[1, step, which, ys], send_z, recv_z,
                      (part, side), device)

    z_copies = {(part, side): z_copy(part, side, sides[side][0])
                for part in range(5) for side in (0, 1)}
    row_copies = [
        remote(p_hbm.at[pl.ds(parity, 2)], got.at[near, 1, pl.ds(parity, 2)],
               send_row, recv_row, 0, far_dev),
        remote(p_hbm.at[pl.ds(1 - parity, 2)], got.at[far, 1, pl.ds(1 - parity, 2)],
               send_row, recv_row, 1, near_dev),
    ]

    z_copies[0, 1].start()
    pl.semaphore_signal(ready, inc=1, device_id=after, device_id_type=MESH)
    row_copies[0].start()
    row_copies[1].start()
    for part in range(1, 5):
        z_copies[part, 1].start()

    forwards = {}
    for side in (0, 1):
        step, start = sides[side][1:]
        for slot, (part, place_x, device) in enumerate((
                (0, near, far_dev), (0, far, near_dev), (1, near, far_dev), (2, near, far_dev),
                (3, far, near_dev), (4, far, near_dev))):
            which, offset, count = parts[part]
            ys = pl.ds(start + offset, count)
            forwards[slot, side] = remote(
                got.at[1, step, which, ys], got.at[place_x, step, which, ys],
                send_fwd, recv_fwd, (slot, side), device)

    def pass_on(part, side):
        z_copies[part, side].wait_recv()
        for slot in ((0, 1), (2,), (3,), (4,), (5,))[part]:
            forwards[slot, side].start()

    def pass_both(part):
        pl.when(jnp.logical_not(bottom))(lambda: pass_on(part, 0))
        pass_on(part, 1)

    @pl.when(bottom)
    def _():
        for part in range(5):
            pass_on(part, 0)

    pl.semaphore_wait(ready, 1)
    for part in range(5):
        z_copies[part, 0].start()

    def load(step_x, step_y, rx):
        first, count = reach(step_y)
        for ry in range(first, first + count):
            h, l = split(got[step_x, step_y, rx, ry])
            high[step_x, step_y, rx, :, 128 * ry : 128 * ry + 128] = h
            low[step_x, step_y, rx, :, 128 * ry : 128 * ry + 128] = l

    def multiply(total, factors, step_x, step_y, rx):
        first, count = reach(step_y)
        factor = factors[step_x, step_y]
        lanes = pl.ds(128 * first, 128 * count)
        target = pl.ds(128 * (first + step_y - 1), 128 * count)
        both = jnp.dot(factor, high[step_x, step_y, rx, :, lanes],
                       preferred_element_type=jnp.float32)
        rest = jnp.dot(factor[:128], low[step_x, step_y, rx, :, lanes],
                       preferred_element_type=jnp.float32)
        total[rx + step_x - 1, :, target] += both[:128] + (both[128:] + rest)

    def add_square(step_x, step_y, rx):
        load(step_x, step_y, rx)
        multiply(square, left, step_x, step_y, rx)

    def add_cube(step_x, step_y, rx):
        multiply(cube, left_cube, step_x, step_y, rx)

    upper = lax.broadcasted_iota(jnp.int32, (128, 128), 0) < 64
    first_half = lax.broadcasted_iota(jnp.int32, (128, 128), 1) < 64

    def keep(index):
        scale = [[kept[a, b, index].astype(jnp.float32) for b in range(2)] for a in range(2)]
        return jnp.where(upper, jnp.where(first_half, scale[0][0], scale[0][1]),
                         jnp.where(first_half, scale[1][0], scale[1][1]))

    def finish_square(target_x):
        for target_y in range(3):
            lanes = pl.ds(128 * target_y, 128)
            value = square[target_x, :, lanes] * keep(3 * target_x + target_y)
            square[target_x, :, lanes] = value
            h, l = split(value)
            left_cube[target_x, target_y, :128] = h
            left_cube[target_x, target_y, 128:] = l

    square[...] = jnp.zeros_like(square)
    cube[...] = jnp.zeros_like(cube)
    own.wait()
    pattern.wait()
    for rx in range(3):
        load(1, 1, rx)
        for ry in range(3):
            lanes = pl.ds(128 * ry, 128)
            left[rx, ry, :128] = high[1, 1, rx, :, lanes]
            left[rx, ry, 128:] = low[1, 1, rx, :, lanes]
    for rx in range(3):
        multiply(square, left, 1, 1, rx)
    row_copies[1].wait_recv()
    add_square(near, 1, 1)
    add_square(near, 1, far)

    pass_both(0)
    for step_y in (2, 0):
        add_square(1, step_y, 1)
    row_copies[0].wait_recv()
    add_square(far, 1, 1)
    add_square(far, 1, near)
    pass_both(1)
    pass_both(2)
    for step_y in (2, 0):
        add_square(1, step_y, far)
    for side in (0, 1):
        forwards[1, side].wait_recv()
    for step_y in (2, 0):
        add_square(near, step_y, 1)
    pass_both(3)
    pass_both(4)
    for step_y in (2, 0):
        add_square(1, step_y, near)
    finish_square(near)
    for step_y in range(3):
        if step_y == 1:
            add_cube(near, 1, far)
        add_cube(near, step_y, 1)
    for side in (0, 1):
        forwards[0, side].wait_recv()
    for step_y in (2, 0):
        add_square(far, step_y, 1)
    finish_square(far)
    for step_y in range(3):
        if step_y == 1:
            add_cube(far, 1, near)
        add_cube(far, step_y, 1)
    for side in (0, 1):
        forwards[4, side].wait_recv()
        forwards[5, side].wait_recv()
    for step_y in (2, 0):
        add_square(near, step_y, far)
        add_cube(near, step_y, far)
    for side in (0, 1):
        forwards[2, side].wait_recv()
        forwards[3, side].wait_recv()
    for step_y in (2, 0):
        add_square(far, step_y, near)
        add_cube(far, step_y, near)
    finish_square(1)
    for step_y in range(3):
        for rx in range(3):
            add_cube(1, step_y, rx)
    for index in range(9):
        lanes = pl.ds(128 * (index % 3), 128)
        value = 3.0 * square[index // 3, :, lanes] - 2.0 * (cube[index // 3, :, lanes] * keep(index))
        out_ref[index] = jnp.where(layer == 0, value[:, :64], value[:, 64:]).T

    for copy in list(z_copies.values()) + row_copies + list(forwards.values()):
        copy.wait_send()


def solution(mesh):
    sizes = dict(mesh.shape)
    rows, cols = sizes["row"], sizes["col"]
    run = min(RUN, cols)

    def whole(*args):
        kernel(rows, cols, run, *args)

    def body(density, retained):
        blocks = density[0, 0].transpose(1, 0, 2).reshape(3, 3, 128, 128)
        kept = retained[0, 0].transpose(0, 2, 1)
        f32, bf16 = jnp.float32, jnp.bfloat16
        dma = pltpu.SemaphoreType.DMA
        result = pl.pallas_call(
            whole,
            out_shape=jax.ShapeDtypeStruct((9, 64, 128), f32),
            in_specs=[pl.BlockSpec(memory_space=pl.ANY), pl.BlockSpec(memory_space=pl.ANY)],
            out_specs=pl.BlockSpec(memory_space=pltpu.VMEM),
            scratch_shapes=[
                pltpu.SMEM((2, 2, 9), jnp.int32),
                pltpu.VMEM((3, 3, 3, 3, 128, 128), f32),
                pltpu.VMEM((3, 3, 3, 128, 384), bf16),
                pltpu.VMEM((3, 3, 3, 128, 384), bf16),
                pltpu.VMEM((3, 3, 256, 128), bf16),
                pltpu.VMEM((3, 3, 256, 128), bf16),
                pltpu.VMEM((3, 128, 384), f32),
                pltpu.VMEM((3, 128, 384), f32),
                dma, dma, pltpu.SemaphoreType.REGULAR, dma((5, 2)), dma((5, 2)), dma((2,)), dma((2,)),
                dma((6, 2)), dma((6, 2)),
            ],
            compiler_params=pltpu.CompilerParams(
                collective_id=0, has_side_effects=True, vmem_limit_bytes=40 << 20),
        )(*(pltpu.with_memory_space_constraint(x, pltpu.HBM) for x in (blocks, kept)))
        return result.transpose(2, 0, 1)[None, None]

    placed = P("row", "col", None, None, None)
    return jax.shard_map(body, mesh=mesh, in_specs=(placed, placed),
                         out_specs=P("row", "col", None, None, "layer"), check_vma=False)
```

```python
import jax
import jax.numpy as jnp
from jax import lax
from jax.experimental import pallas as pl
from jax.experimental.pallas import tpu as pltpu
from jax.sharding import PartitionSpec as P

MESH = pl.DeviceIdType.MESH
RUN = 8


def reach(step):
    return max(0, 1 - step), 3 - abs(step - 1)


def split(value):
    high = value.astype(jnp.bfloat16)
    low = (value - high.astype(jnp.float32)).astype(jnp.bfloat16)
    return high, low


def kernel(rows, cols, run, p_hbm, kept_hbm, out_ref, kept, got, high, low, left, left_cube, square,
           cube, local_sem, kept_sem, ready, send_z, recv_z, send_row, recv_row, send_fwd, recv_fwd):
    row, col, layer = lax.axis_index("row"), lax.axis_index("col"), lax.axis_index("layer")
    parity = lax.rem(row, 2)
    far, near = 2 * parity, 2 - 2 * parity
    far_dev = (lax.rem(row + far - 1 + rows, rows), col, layer)
    near_dev = (lax.rem(row + near - 1 + rows, rows), col, layer)
    place = lax.rem(col, run)
    after = (row, lax.rem(col + 1, cols), lax.rem(layer + lax.div(place + 1, run), 2))
    before = (row, lax.rem(col + cols - 1, cols), lax.rem(layer + lax.div(run - place, run), 2))

    late = jnp.logical_and(layer == 0, jnp.logical_and(col == 0, row < 2))

    barrier = pltpu.get_barrier_semaphore()
    for device in (before, far_dev, near_dev):
        pl.semaphore_signal(barrier, inc=1, device_id=device, device_id_type=MESH)

    own = pltpu.make_async_copy(p_hbm, got.at[1, 1], local_sem)
    own.start()
    pattern = pltpu.make_async_copy(kept_hbm, kept, kept_sem)
    pattern.start()
    pl.semaphore_wait(barrier, 3)

    def remote(src, dst, sems, rsems, place, device):
        return pltpu.make_async_remote_copy(
            src_ref=src, dst_ref=dst, send_sem=sems.at[place], recv_sem=rsems.at[place],
            device_id=device, device_id_type=MESH)

    parts = ((1, 0, 2), (far, 0, 1), (far, 1, 1), (near, 0, 1), (near, 1, 1))
    sides = ((before, 2, 0), (after, 0, 1))

    def z_copy(part, side, device):
        which, offset, count = parts[part]
        step, start = sides[side][1:]
        ys = pl.ds(start + offset, count)
        return remote(p_hbm.at[which, ys], got.at[1, step, which, ys], send_z, recv_z,
                      (part, side), device)

    z_copies = {(part, side): z_copy(part, side, sides[side][0])
                for part in range(5) for side in (0, 1)}
    row_copies = [
        remote(p_hbm.at[pl.ds(parity, 2)], got.at[near, 1, pl.ds(parity, 2)],
               send_row, recv_row, 0, far_dev),
        remote(p_hbm.at[pl.ds(1 - parity, 2)], got.at[far, 1, pl.ds(1 - parity, 2)],
               send_row, recv_row, 1, near_dev),
    ]

    pl.semaphore_signal(ready, inc=1, device_id=after, device_id_type=MESH)
    z_copies[0, 1].start()
    row_copies[0].start()
    row_copies[1].start()
    for part in range(1, 5):
        z_copies[part, 1].start()

    forwards = {}
    for side in (0, 1):
        step, start = sides[side][1:]
        for slot, (part, place_x, device) in enumerate((
                (0, near, far_dev), (0, far, near_dev), (1, near, far_dev), (2, near, far_dev),
                (3, far, near_dev), (4, far, near_dev))):
            which, offset, count = parts[part]
            ys = pl.ds(start + offset, count)
            forwards[slot, side] = remote(
                got.at[1, step, which, ys], got.at[place_x, step, which, ys],
                send_fwd, recv_fwd, (slot, side), device)

    def pass_on(part, side):
        z_copies[part, side].wait_recv()
        for slot in ((0, 1), (2,), (3,), (4,), (5,))[part]:
            forwards[slot, side].start()

    def load(step_x, step_y, rx):
        first, count = reach(step_y)
        for ry in range(first, first + count):
            h, l = split(got[step_x, step_y, rx, ry])
            high[step_x, step_y, rx, :, 128 * ry : 128 * ry + 128] = h
            low[step_x, step_y, rx, :, 128 * ry : 128 * ry + 128] = l

    def multiply(total, factors, step_x, step_y, rx):
        first, count = reach(step_y)
        factor = factors[step_x, step_y]
        lanes = pl.ds(128 * first, 128 * count)
        target = pl.ds(128 * (first + step_y - 1), 128 * count)
        both = jnp.dot(factor, high[step_x, step_y, rx, :, lanes],
                       preferred_element_type=jnp.float32)
        rest = jnp.dot(factor[:128], low[step_x, step_y, rx, :, lanes],
                       preferred_element_type=jnp.float32)
        total[rx + step_x - 1, :, target] += both[:128] + (both[128:] + rest)

    def add_square(step_x, step_y, rx):
        load(step_x, step_y, rx)
        multiply(square, left, step_x, step_y, rx)

    def add_cube(step_x, step_y, rx):
        multiply(cube, left_cube, step_x, step_y, rx)

    upper = lax.broadcasted_iota(jnp.int32, (128, 128), 0) < 64
    first_half = lax.broadcasted_iota(jnp.int32, (128, 128), 1) < 64

    def keep(index):
        scale = [[kept[a, b, index].astype(jnp.float32) for b in range(2)] for a in range(2)]
        return jnp.where(upper, jnp.where(first_half, scale[0][0], scale[0][1]),
                         jnp.where(first_half, scale[1][0], scale[1][1]))

    def finish_square(target_x):
        for target_y in range(3):
            lanes = pl.ds(128 * target_y, 128)
            value = square[target_x, :, lanes] * keep(3 * target_x + target_y)
            square[target_x, :, lanes] = value
            h, l = split(value)
            left_cube[target_x, target_y, :128] = h
            left_cube[target_x, target_y, 128:] = l

    square[...] = jnp.zeros_like(square)
    cube[...] = jnp.zeros_like(cube)
    own.wait()
    pattern.wait()
    for rx in range(3):
        load(1, 1, rx)
        for ry in range(3):
            lanes = pl.ds(128 * ry, 128)
            left[rx, ry, :128] = high[1, 1, rx, :, lanes]
            left[rx, ry, 128:] = low[1, 1, rx, :, lanes]
    for rx in range(3):
        multiply(square, left, 1, 1, rx)
    row_copies[1].wait_recv()
    add_square(near, 1, 1)
    add_square(near, 1, far)

    pl.semaphore_wait(ready, 1)
    for part in range(5):
        z_copies[part, 0].start()

    @pl.when(late)
    def _():
        for part in range(5):
            pass_on(part, 0)
            pass_on(part, 1)

    @pl.when(jnp.logical_not(late))
    def _():
        for part in range(5):
            pass_on(part, 0)

    def pass_late(part):
        pl.when(jnp.logical_not(late))(lambda: pass_on(part, 1))

    row_copies[0].wait_recv()
    for step_x, rx in ((far, 1), (far, near)):
        add_square(step_x, 1, rx)
    for rx in range(3):
        add_square(1, 2, rx)
    for slot in range(6):
        forwards[slot, 0].wait_recv()
    for step_x, rx in ((near, 1), (near, far), (far, 1), (far, near)):
        add_square(step_x, 2, rx)
    for part in range(3):
        pass_late(part)
    add_square(1, 0, 1)
    add_square(1, 0, far)
    forwards[0, 1].wait_recv()
    add_square(far, 0, 1)
    finish_square(far)
    pass_late(3)
    for step_y, rx in ((0, 1), (1, 1), (2, 1), (1, near), (2, near)):
        add_cube(far, step_y, rx)
    pass_late(4)
    forwards[1, 1].wait_recv()
    add_square(near, 0, 1)
    add_square(1, 0, near)
    finish_square(near)
    for step_y, rx in ((0, 1), (1, 1), (2, 1), (1, far), (2, far)):
        add_cube(near, step_y, rx)
    for slots, step_x, rx in (((2, 3), far, near), ((4, 5), near, far)):
        for slot in slots:
            forwards[slot, 1].wait_recv()
        add_square(step_x, 0, rx)
        add_cube(step_x, 0, rx)
    finish_square(1)
    for step_y in range(3):
        for rx in range(3):
            add_cube(1, step_y, rx)
    for index in range(9):
        lanes = pl.ds(128 * (index % 3), 128)
        value = 3.0 * square[index // 3, :, lanes] - 2.0 * (cube[index // 3, :, lanes] * keep(index))
        out_ref[index] = jnp.where(layer == 0, value[:, :64], value[:, 64:]).T

    for copy in list(z_copies.values()) + row_copies + list(forwards.values()):
        copy.wait_send()


def solution(mesh):
    sizes = dict(mesh.shape)
    rows, cols = sizes["row"], sizes["col"]
    run = min(RUN, cols)

    def whole(*args):
        kernel(rows, cols, run, *args)

    def body(density, retained):
        blocks = density[0, 0].transpose(1, 0, 2).reshape(3, 3, 128, 128)
        kept = retained[0, 0].transpose(0, 2, 1)
        f32, bf16 = jnp.float32, jnp.bfloat16
        dma = pltpu.SemaphoreType.DMA
        result = pl.pallas_call(
            whole,
            out_shape=jax.ShapeDtypeStruct((9, 64, 128), f32),
            in_specs=[pl.BlockSpec(memory_space=pl.ANY), pl.BlockSpec(memory_space=pl.ANY)],
            out_specs=pl.BlockSpec(memory_space=pltpu.VMEM),
            scratch_shapes=[
                pltpu.SMEM((2, 2, 9), jnp.int32),
                pltpu.VMEM((3, 3, 3, 3, 128, 128), f32),
                pltpu.VMEM((3, 3, 3, 128, 384), bf16),
                pltpu.VMEM((3, 3, 3, 128, 384), bf16),
                pltpu.VMEM((3, 3, 256, 128), bf16),
                pltpu.VMEM((3, 3, 256, 128), bf16),
                pltpu.VMEM((3, 128, 384), f32),
                pltpu.VMEM((3, 128, 384), f32),
                dma, dma, pltpu.SemaphoreType.REGULAR, dma((5, 2)), dma((5, 2)), dma((2,)), dma((2,)),
                dma((6, 2)), dma((6, 2)),
            ],
            compiler_params=pltpu.CompilerParams(
                collective_id=0, has_side_effects=True, vmem_limit_bytes=40 << 20),
        )(*(pltpu.with_memory_space_constraint(x, pltpu.HBM) for x in (blocks, kept)))
        return result.transpose(2, 0, 1)[None, None]

    placed = P("row", "col", None, None, None)
    return jax.shard_map(body, mesh=mesh, in_specs=(placed, placed),
                         out_specs=P("row", "col", None, None, "layer"), check_vma=False)
```

```python
import jax
import jax.numpy as jnp
from jax import lax
from jax.experimental import pallas as pl
from jax.experimental.pallas import tpu as pltpu
from jax.sharding import PartitionSpec as P

MESH = pl.DeviceIdType.MESH
RUN = 8


def reach(step):
    return max(0, 1 - step), 3 - abs(step - 1)


def split(value):
    high = value.astype(jnp.bfloat16)
    low = (value - high.astype(jnp.float32)).astype(jnp.bfloat16)
    return high, low


def kernel(rows, cols, run, p_hbm, kept_hbm, out_ref, kept, got, high, low, left, left_cube, square,
           cube, local_sem, kept_sem, ready, send_z, recv_z, send_row, recv_row, send_fwd, recv_fwd):
    row, col, layer = lax.axis_index("row"), lax.axis_index("col"), lax.axis_index("layer")
    parity = lax.rem(row, 2)
    far, near = 2 * parity, 2 - 2 * parity
    far_dev = (lax.rem(row + far - 1 + rows, rows), col, layer)
    near_dev = (lax.rem(row + near - 1 + rows, rows), col, layer)
    place = lax.rem(col, run)
    after = (row, lax.rem(col + 1, cols), lax.rem(layer + lax.div(place + 1, run), 2))
    before = (row, lax.rem(col + cols - 1, cols), lax.rem(layer + lax.div(run - place, run), 2))

    bottom = jnp.logical_and(jnp.logical_and(layer == 0, place == 0), row + col > 1)

    barrier = pltpu.get_barrier_semaphore()
    for device in (before, far_dev, near_dev):
        pl.semaphore_signal(barrier, inc=1, device_id=device, device_id_type=MESH)

    own = pltpu.make_async_copy(p_hbm, got.at[1, 1], local_sem)
    own.start()
    pattern = pltpu.make_async_copy(kept_hbm, kept, kept_sem)
    pattern.start()
    pl.semaphore_wait(barrier, 3)

    def remote(src, dst, sems, rsems, place, device):
        return pltpu.make_async_remote_copy(
            src_ref=src, dst_ref=dst, send_sem=sems.at[place], recv_sem=rsems.at[place],
            device_id=device, device_id_type=MESH)

    parts = ((1, 0, 2), (far, 0, 1), (far, 1, 1), (near, 0, 1), (near, 1, 1))
    sides = ((before, 2, 0), (after, 0, 1))

    def z_copy(part, side, device):
        which, offset, count = parts[part]
        step, start = sides[side][1:]
        ys = pl.ds(start + offset, count)
        return remote(p_hbm.at[which, ys], got.at[1, step, which, ys], send_z, recv_z,
                      (part, side), device)

    z_copies = {(part, side): z_copy(part, side, sides[side][0])
                for part in range(5) for side in (0, 1)}
    row_copies = [
        remote(p_hbm.at[pl.ds(parity, 2)], got.at[near, 1, pl.ds(parity, 2)],
               send_row, recv_row, 0, far_dev),
        remote(p_hbm.at[pl.ds(1 - parity, 2)], got.at[far, 1, pl.ds(1 - parity, 2)],
               send_row, recv_row, 1, near_dev),
    ]

    pl.semaphore_signal(ready, inc=1, device_id=after, device_id_type=MESH)
    z_copies[0, 1].start()
    row_copies[0].start()
    row_copies[1].start()
    for part in range(1, 5):
        z_copies[part, 1].start()

    forwards = {}
    for side in (0, 1):
        step, start = sides[side][1:]
        for slot, (part, place_x, device) in enumerate((
                (0, near, far_dev), (0, far, near_dev), (1, near, far_dev), (2, near, far_dev),
                (3, far, near_dev), (4, far, near_dev))):
            which, offset, count = parts[part]
            ys = pl.ds(start + offset, count)
            forwards[slot, side] = remote(
                got.at[1, step, which, ys], got.at[place_x, step, which, ys],
                send_fwd, recv_fwd, (slot, side), device)

    def pass_on(part, side):
        z_copies[part, side].wait_recv()
        for slot in ((0, 1), (2,), (3,), (4,), (5,))[part]:
            forwards[slot, side].start()

    def pass_both(part):
        pl.when(jnp.logical_not(bottom))(lambda: pass_on(part, 0))
        pass_on(part, 1)

    pl.semaphore_wait(ready, 1)
    for part in range(5):
        z_copies[part, 0].start()

    @pl.when(bottom)
    def _():
        for part in range(5):
            pass_on(part, 0)

    def load(step_x, step_y, rx):
        first, count = reach(step_y)
        for ry in range(first, first + count):
            h, l = split(got[step_x, step_y, rx, ry])
            high[step_x, step_y, rx, :, 128 * ry : 128 * ry + 128] = h
            low[step_x, step_y, rx, :, 128 * ry : 128 * ry + 128] = l

    def multiply(total, factors, step_x, step_y, rx):
        first, count = reach(step_y)
        factor = factors[step_x, step_y]
        lanes = pl.ds(128 * first, 128 * count)
        target = pl.ds(128 * (first + step_y - 1), 128 * count)
        both = jnp.dot(factor, high[step_x, step_y, rx, :, lanes],
                       preferred_element_type=jnp.float32)
        rest = jnp.dot(factor[:128], low[step_x, step_y, rx, :, lanes],
                       preferred_element_type=jnp.float32)
        total[rx + step_x - 1, :, target] += both[:128] + (both[128:] + rest)

    def add_square(step_x, step_y, rx):
        load(step_x, step_y, rx)
        multiply(square, left, step_x, step_y, rx)

    def add_cube(step_x, step_y, rx):
        multiply(cube, left_cube, step_x, step_y, rx)

    upper = lax.broadcasted_iota(jnp.int32, (128, 128), 0) < 64
    first_half = lax.broadcasted_iota(jnp.int32, (128, 128), 1) < 64

    def keep(index):
        scale = [[kept[a, b, index].astype(jnp.float32) for b in range(2)] for a in range(2)]
        return jnp.where(upper, jnp.where(first_half, scale[0][0], scale[0][1]),
                         jnp.where(first_half, scale[1][0], scale[1][1]))

    def finish_square(target_x):
        for target_y in range(3):
            lanes = pl.ds(128 * target_y, 128)
            value = square[target_x, :, lanes] * keep(3 * target_x + target_y)
            square[target_x, :, lanes] = value
            h, l = split(value)
            left_cube[target_x, target_y, :128] = h
            left_cube[target_x, target_y, 128:] = l

    square[...] = jnp.zeros_like(square)
    cube[...] = jnp.zeros_like(cube)
    own.wait()
    pattern.wait()
    for rx in range(3):
        load(1, 1, rx)
        for ry in range(3):
            lanes = pl.ds(128 * ry, 128)
            left[rx, ry, :128] = high[1, 1, rx, :, lanes]
            left[rx, ry, 128:] = low[1, 1, rx, :, lanes]
    for rx in range(3):
        multiply(square, left, 1, 1, rx)
    row_copies[1].wait_recv()
    add_square(near, 1, 1)
    add_square(near, 1, far)

    pass_both(0)
    for step_y in (2, 0):
        add_square(1, step_y, 1)
    row_copies[0].wait_recv()
    add_square(far, 1, 1)
    add_square(far, 1, near)
    pass_both(1)
    pass_both(2)
    for step_y in (2, 0):
        add_square(1, step_y, far)
    for side in (0, 1):
        forwards[1, side].wait_recv()
    for step_y in (2, 0):
        add_square(near, step_y, 1)
    pass_both(3)
    pass_both(4)
    for step_y in (2, 0):
        add_square(1, step_y, near)
    finish_square(near)
    for step_y in range(3):
        if step_y == 1:
            add_cube(near, 1, far)
        add_cube(near, step_y, 1)
    for side in (0, 1):
        forwards[0, side].wait_recv()
    for step_y in (2, 0):
        add_square(far, step_y, 1)
    finish_square(far)
    for step_y in range(3):
        if step_y == 1:
            add_cube(far, 1, near)
        add_cube(far, step_y, 1)
    for side in (0, 1):
        forwards[4, side].wait_recv()
        forwards[5, side].wait_recv()
    for step_y in (2, 0):
        add_square(near, step_y, far)
        add_cube(near, step_y, far)
    for side in (0, 1):
        forwards[2, side].wait_recv()
        forwards[3, side].wait_recv()
    for step_y in (2, 0):
        add_square(far, step_y, near)
        add_cube(far, step_y, near)
    finish_square(1)
    for step_y in range(3):
        for rx in range(3):
            add_cube(1, step_y, rx)
    for index in range(9):
        lanes = pl.ds(128 * (index % 3), 128)
        value = 3.0 * square[index // 3, :, lanes] - 2.0 * (cube[index // 3, :, lanes] * keep(index))
        out_ref[index] = jnp.where(layer == 0, value[:, :64], value[:, 64:]).T

    for copy in list(z_copies.values()) + row_copies + list(forwards.values()):
        copy.wait_send()


def solution(mesh):
    sizes = dict(mesh.shape)
    rows, cols = sizes["row"], sizes["col"]
    run = min(RUN, cols)

    def whole(*args):
        kernel(rows, cols, run, *args)

    def body(density, retained):
        blocks = density[0, 0].transpose(1, 0, 2).reshape(3, 3, 128, 128)
        kept = retained[0, 0].transpose(0, 2, 1)
        f32, bf16 = jnp.float32, jnp.bfloat16
        dma = pltpu.SemaphoreType.DMA
        result = pl.pallas_call(
            whole,
            out_shape=jax.ShapeDtypeStruct((9, 64, 128), f32),
            in_specs=[pl.BlockSpec(memory_space=pl.ANY), pl.BlockSpec(memory_space=pl.ANY)],
            out_specs=pl.BlockSpec(memory_space=pltpu.VMEM),
            scratch_shapes=[
                pltpu.SMEM((2, 2, 9), jnp.int32),
                pltpu.VMEM((3, 3, 3, 3, 128, 128), f32),
                pltpu.VMEM((3, 3, 3, 128, 384), bf16),
                pltpu.VMEM((3, 3, 3, 128, 384), bf16),
                pltpu.VMEM((3, 3, 256, 128), bf16),
                pltpu.VMEM((3, 3, 256, 128), bf16),
                pltpu.VMEM((3, 128, 384), f32),
                pltpu.VMEM((3, 128, 384), f32),
                dma, dma, pltpu.SemaphoreType.REGULAR, dma((5, 2)), dma((5, 2)), dma((2,)), dma((2,)),
                dma((6, 2)), dma((6, 2)),
            ],
            compiler_params=pltpu.CompilerParams(
                collective_id=0, has_side_effects=True, vmem_limit_bytes=40 << 20),
        )(*(pltpu.with_memory_space_constraint(x, pltpu.HBM) for x in (blocks, kept)))
        return result.transpose(2, 0, 1)[None, None]

    placed = P("row", "col", None, None, None)
    return jax.shard_map(body, mesh=mesh, in_specs=(placed, placed),
                         out_specs=P("row", "col", None, None, "layer"), check_vma=False)
```
